32 devices in a mesh: row: 16 (over z, x, core), col: 2 (over y).
Axes of the slice: x: 2, y: 2, z: 4, core: 2. Of those that a mesh axis runs over, the one named last changes fastest.
Arguments:
- base_velocity: bfloat16 [3, 512, 256, 384], P(None, 'row', 'col'), may hold values from -6 to 6
- velocity_step: bfloat16 [3, 512, 256, 384], P(None, 'row', 'col'), may hold values from -6 to 6
- adjoint_velocity: bfloat16 [3, 512, 256, 384], P(None, 'row', 'col'), may hold values from -6 to 6
- increment_weight: float32 [1], replicated, may hold values from 0.3 to 0.9
- streamwise_first: bfloat16 [3, 128, 128], replicated, may hold values from -0.3125 to 0.3125
- streamwise_second: bfloat16 [3, 128, 128], replicated, may hold values from -0.3125 to 0.3125
- normal_first: bfloat16 [512, 512], replicated, may hold values from -0.25 to 0.25
- normal_second: bfloat16 [512, 512], replicated, may hold values from -0.25 to 0.25
- spanwise_first: bfloat16 [256, 256], replicated, may hold values from -0.375 to 0.375
- spanwise_second: bfloat16 [256, 256], replicated, may hold values from -0.375 to 0.375
- wall_profile: float32 [2, 512], P(None, 'row'), may hold values from 0.5 to 1.5
Outputs:
- adjoint_tendency: bfloat16 [3, 512, 256, 384], P(None, 'row', 'col')
The draws below stay inside these ranges and needn't reach their ends.
All inputs are finite; a program needn't handle non-finite values.
Results may differ from the reference program's by a relative error of at most 0.012.
Values may be sent and summed in bfloat16 or wider, within the bound.
No kernel may reach another device: no remote copies, remote signals or barrier semaphores. Data moves between devices by JAX's collectives and lax.ppermute only.
A program may use at most 448 MiB of HBM per device.

```python
import jax
import jax.numpy as jnp
from jax import lax

NX = 384
NY = 512
NZ = 256
BLOCK = 128


def shard_levels(own_key, dims, shards, low, largest):
    factor_of, own = 1.0, jax.random.fold_in(own_key, 6)
    for dim, parts in shards:
        steps = jnp.exp(jax.random.uniform(jax.random.fold_in(own, dim), (parts,), jnp.float32, low / len(shards), largest / len(shards)))
        factor_of = factor_of * jnp.repeat(steps, dims[dim] // parts).reshape([-1 if axis == dim else 1 for axis in range(len(dims))])
    return factor_of


def bell_draw(stream_key, extent, width, reach, cuts=(), kind=jnp.bfloat16):
    result = jax.random.normal(stream_key, extent, jnp.float32) * width
    if len(cuts) > 0:
        result = shard_levels(stream_key, extent, cuts, -0.22, 0.18) * result
    return jnp.clip(result, min=-reach, max=reach).astype(kind)


def setup_inputs(seed: int = 0) -> dict:
    streams_of = jax.random.split(jax.random.key(seed), 12)
    base_velocity = bell_draw(streams_of[0], (3, NY, NZ, NX), 1.0, 6.0, ((1, 16), (2, 2)))
    velocity_step = bell_draw(streams_of[1], (3, NY, NZ, NX), 1.0, 6.0, ((1, 16), (2, 2)))
    adjoint_velocity = bell_draw(streams_of[2], (3, NY, NZ, NX), 1.0, 6.0, ((1, 16), (2, 2)))
    increment_weight = jnp.clip(jax.random.uniform(streams_of[3], (1,), jnp.float32, 0.3, 0.9), 0.3, 0.9)
    streamwise_first = bell_draw(streams_of[4], (3, BLOCK, BLOCK), (3 * BLOCK) ** -0.5, 0.3125)
    streamwise_second = bell_draw(streams_of[5], (3, BLOCK, BLOCK), (3 * BLOCK) ** -0.5, 0.3125)
    normal_first = bell_draw(streams_of[6], (NY, NY), NY ** -0.5, 0.25)
    normal_second = bell_draw(streams_of[7], (NY, NY), NY ** -0.5, 0.25)
    spanwise_first = bell_draw(streams_of[8], (NZ, NZ), NZ ** -0.5, 0.375)
    spanwise_second = bell_draw(streams_of[9], (NZ, NZ), NZ ** -0.5, 0.375)
    wall_profile = jnp.clip(0.5 + 1.0 * jax.random.uniform(streams_of[10], (2, NY), jnp.float32) ** shard_levels(streams_of[10], (2, NY), ((1, 16),), -0.2, 0.2), 0.5, 1.5)
    return dict(base_velocity=base_velocity, velocity_step=velocity_step, adjoint_velocity=adjoint_velocity, increment_weight=increment_weight, streamwise_first=streamwise_first, streamwise_second=streamwise_second, normal_first=normal_first, normal_second=normal_second, spanwise_first=spanwise_first, spanwise_second=spanwise_second, wall_profile=wall_profile)


def along_stream(field, operators):
    block_width = operators[0].shape[1]
    block_count = field.shape[-1] // block_width
    tiles = field.reshape(field.shape[:-1] + (block_count, block_width))
    joined = jnp.concatenate([blocks[k] for blocks in operators for k in range(3)], axis=1)
    product = jnp.dot(tiles, joined, preferred_element_type=jnp.float32)
    results = []
    for number in range(len(operators)):
        start = 3 * number * block_width
        lower = product[..., start:start + block_width]
        middle = product[..., start + block_width:start + 2 * block_width]
        upper = product[..., start + 2 * block_width:start + 3 * block_width]
        combined = jnp.roll(lower, 1, axis=-2) + middle + jnp.roll(upper, -1, axis=-2)
        results.append(combined.reshape(field.shape))
    return results


def along_normal(field, operator):
    return jnp.einsum('wy,cyzx->cwzx', operator.astype(jnp.float32), field.astype(jnp.float32), precision=lax.Precision.HIGHEST)


def along_span(field, operator):
    return jnp.einsum('vz,cyzx->cyvx', operator.astype(jnp.float32), field.astype(jnp.float32), precision=lax.Precision.HIGHEST)


def component_mask(which, ndim):
    return (jnp.arange(3) == which).astype(jnp.float32).reshape((3,) + (1,) * (ndim - 1))


def adjoint_terms(velocity, adjoint, slope_velocity, slope_adjoint, curve_adjoint, direction):
    cross = jnp.sum(adjoint.astype(jnp.float32) * slope_velocity, axis=0)
    advect = velocity[direction].astype(jnp.float32)[None] * slope_adjoint
    return curve_adjoint - advect + component_mask(direction, adjoint.ndim) * cross[None]


def reference(base_velocity, velocity_step, adjoint_velocity, increment_weight, streamwise_first, streamwise_second, normal_first, normal_second, spanwise_first, spanwise_second, wall_profile):
    velocity = (base_velocity.astype(jnp.float32) + increment_weight[0] * velocity_step.astype(jnp.float32)).astype(jnp.bfloat16)
    slab_width = 32
    slab_count = NX // slab_width

    def slab_work(slab):
        start = (slab * slab_width).astype(jnp.int32)
        speed = lax.dynamic_slice_in_dim(velocity, start, slab_width, 3)
        adjoint = lax.dynamic_slice_in_dim(adjoint_velocity, start, slab_width, 3)
        slope_speed = along_normal(speed, normal_first)
        normal_term = adjoint_terms(speed, adjoint, slope_speed, along_normal(adjoint, normal_first), along_normal(adjoint, normal_second), 1).astype(jnp.bfloat16)
        span_term = adjoint_terms(speed, adjoint, along_span(speed, spanwise_first), along_span(adjoint, spanwise_first), along_span(adjoint, spanwise_second), 2).astype(jnp.bfloat16)
        far_terms = (normal_term.astype(jnp.float32) + span_term.astype(jnp.float32)).astype(jnp.bfloat16)
        strip = jnp.stack([slope_speed[0, 0], slope_speed[0, -1]]).astype(jnp.bfloat16)
        return far_terms, strip

    far_slabs, strip_slabs = lax.map(slab_work, jnp.arange(slab_count, dtype=jnp.int32))
    far_terms = jnp.moveaxis(far_slabs, 0, 3).reshape((3, NY, NZ, NX))
    wall_shear = jnp.moveaxis(strip_slabs, 0, 2).reshape((2, NZ, NX))
    (shear_slope,) = along_stream(wall_shear, [streamwise_first])

    def row_work(items):
        speed, adjoint, far_row, profile = items
        (slope_speed,) = along_stream(speed, [streamwise_first])
        slope_adjoint, curve_adjoint = along_stream(adjoint, [streamwise_first, streamwise_second])
        near = adjoint_terms(speed, adjoint, slope_speed, slope_adjoint, curve_adjoint, 0)
        forcing = profile[0] * shear_slope[0] + profile[1] * shear_slope[1]
        total = near + far_row.astype(jnp.float32) + component_mask(0, 3) * forcing[None]
        return total.astype(jnp.bfloat16)

    rows = lax.map(row_work, (jnp.moveaxis(velocity, 1, 0), jnp.moveaxis(adjoint_velocity, 1, 0), jnp.moveaxis(far_terms, 1, 0), wall_profile.T))
    return jnp.moveaxis(rows, 0, 1)
```

```python
import functools

import jax
import jax.numpy as jnp
from jax import lax
from jax.experimental import pallas as pl
from jax.experimental.pallas import tpu as pltpu
from jax.sharding import PartitionSpec as P

F32 = jnp.float32
BF16 = jnp.bfloat16
LANES = 128
VMEM_LIMIT = 56 * 1024 * 1024


def params():
    return pltpu.CompilerParams(vmem_limit_bytes=VMEM_LIMIT)


def cost(flops, bytes_accessed):
    return pl.CostEstimate(flops=flops, bytes_accessed=bytes_accessed, transcendentals=0)


def resident(shape):
    return pl.BlockSpec(shape, lambda *_: (0,) * len(shape))


def unread():
    return pl.BlockSpec(memory_space=pl.ANY)


def mixed(weight, base, step):
    return (base.astype(F32) + weight * step.astype(F32)).astype(BF16)


def prepare_kernel(weight_ref, base_ref, step_ref, adjoint_ref, *refs):
    sent_ref, turned = refs[-2:]
    rows, planes, cells = base_ref.shape[1:]
    weight = weight_ref[0]
    for part in range(cells // LANES):
        lanes = pl.ds(part * LANES, LANES)
        for field in range(6):
            component = field % 3
            if field < 3:
                value = mixed(weight, base_ref[component, :, :, lanes], step_ref[component, :, :, lanes])
                value = value.astype(F32)
            else:
                value = adjoint_ref[component, :, :, lanes].astype(F32)
            turned[field % 2] = value.reshape(rows * planes, LANES)
            for plane in range(planes):
                sent_ref[plane, field, :, lanes] = turned[
                    field % 2, pl.ds(plane, rows, stride=planes), :
                ].astype(BF16)


def prepare(weight, base, step, adjoint, earlier, first, count, width):
    _, rows, _, cells = base.shape
    start = first // width
    source = pl.BlockSpec((3, rows, width, cells), lambda i: (0, 0, start + i, 0))
    scalars = pl.BlockSpec(memory_space=pltpu.SMEM)
    return pl.pallas_call(
        prepare_kernel,
        grid=(count // width,),
        in_specs=[scalars, source, source, source] + [unread()] * len(earlier),
        out_specs=pl.BlockSpec((width, 6, rows, cells), lambda i: (i, 0, 0, 0)),
        out_shape=jax.ShapeDtypeStruct((count, 6, rows, cells), BF16),
        scratch_shapes=[pltpu.VMEM((2, rows * width, LANES), F32)],
        compiler_params=params(),
        cost_estimate=cost(0, 30 * count * rows * cells),
        name="prepare",
    )(weight, base, step, adjoint, *earlier)


def strip_rows(planes):
    return next(total for total in range(8, 16 * planes + 8, 8) if total % planes == 0 and total >= 2 * planes)


def normal_kernel(planes, first_ref, second_ref, lines_ref, *refs):
    out_ref, strips = refs[-2:]
    owners, _, _, rows, cells = lines_ref.shape
    lines = owners * rows
    plane = pl.program_id(0)

    def whole(field):
        return lines_ref[:, 0, field].reshape(lines, cells)

    @pl.when(plane == 0)
    def _():
        strips[...] = jnp.zeros_like(strips)

    first = first_ref[...]
    second = second_ref[...]
    cross = None
    for component in range(3):
        slope = jnp.dot(first, whole(component), preferred_element_type=F32)
        if component == 0:
            place = plane * (strips.shape[0] // planes)
            strips[pl.ds(place, 1), :] = slope[:1]
            strips[pl.ds(place + 1, 1), :] = slope[lines - 1 :]
        term = whole(3 + component).astype(F32) * slope
        cross = term if cross is None else cross + term
    speed = whole(1).astype(F32)
    for component in range(3):
        field = whole(3 + component)
        slope = jnp.dot(first, field, preferred_element_type=F32)
        term = jnp.dot(second, field, preferred_element_type=F32) - speed * slope
        if component == 1:
            term = term + cross
        place = pl.multiple_of((3 * plane + component) * rows, rows)
        out_ref[:, pl.ds(place, rows), :] = term.astype(BF16).reshape(owners, rows, cells)

    @pl.when(plane == planes - 1)
    def _():
        last = strips[...].astype(BF16)
        for owner in range(owners):
            out_ref[owner, 3 * planes * rows :, :] = last


def normal(first_op, second_op, received, earlier):
    owners, planes, _, rows, cells = received.shape
    lines = owners * rows
    length = 3 * planes * rows + strip_rows(planes)
    return pl.pallas_call(
        functools.partial(normal_kernel, planes),
        grid=(planes,),
        in_specs=[
            resident((lines, lines)),
            resident((lines, lines)),
            pl.BlockSpec((owners, 1, 6, rows, cells), lambda p: (0, p, 0, 0, 0)),
        ]
        + [unread()] * len(earlier),
        out_specs=resident((owners, length, cells)),
        out_shape=jax.ShapeDtypeStruct((owners, length, cells), BF16),
        scratch_shapes=[pltpu.VMEM((strip_rows(planes), cells), F32)],
        compiler_params=params(),
        cost_estimate=cost(18 * planes * lines * lines * cells, 18 * planes * lines * cells),
        name="normal",
    )(first_op, second_op, received, *earlier)


def near_kernel(parts, weight_ref, stream_ref, curve_ref, cross_ref, base_ref, step_ref, *refs):
    adjoint_refs = refs[:parts]
    near_ref = refs[-parts]
    partial_refs = refs[len(refs) - parts + 1 :]
    _, _, planes, cells = base_ref.shape
    weight = weight_ref[0]
    stream = stream_ref[...]
    curve = curve_ref[...]
    speeds = [mixed(weight, base_ref[c, 0], step_ref[c, 0]) for c in range(3)]
    adjoints = [[ref[c, 0] for ref in adjoint_refs] for c in range(3)]
    stream_cross = None
    span_cross = [None] * parts
    for c in range(3):
        slope = jnp.dot(speeds[c], stream[:, :cells], preferred_element_type=F32)
        term = adjoints[c][0].astype(F32) * slope
        stream_cross = term if stream_cross is None else stream_cross + term
        slopes = jnp.dot(cross_ref[...], speeds[c], preferred_element_type=F32)
        for part in range(parts):
            term = adjoints[c][part].astype(F32) * slopes[part * planes : (part + 1) * planes]
            span_cross[part] = term if span_cross[part] is None else span_cross[part] + term
    for part in range(1, parts):
        partial_refs[part - 1][0] = span_cross[part].astype(BF16)
    for c in range(3):
        along = jnp.dot(adjoints[c][0], stream, preferred_element_type=F32)
        total = along[:, cells:] - speeds[0].astype(F32) * along[:, :cells]
        across = jnp.dot(curve, jnp.concatenate(adjoints[c], axis=0), preferred_element_type=F32)
        total += across[planes:] - speeds[2].astype(F32) * across[:planes]
        if c == 0:
            total += stream_cross
        if c == 2:
            total += span_cross[0]
        near_ref[c, 0] = total.astype(BF16)


def near(weight, stream, curve, cross, base, step, own, others, previous, first):
    _, rows, planes, cells = base.shape
    parts = 1 + len(others)
    count = rows if not others else others[0].shape[1]
    row_of = pl.BlockSpec((3, 1, planes, cells), lambda i: (0, first + i, 0, 0))
    row_one = pl.BlockSpec((1, planes, cells), lambda i: (first + i, 0, 0))
    scalars = pl.BlockSpec(memory_space=pltpu.SMEM)
    operands = [weight, stream, curve, cross, base, step, own, *others]
    aliases = {}
    if previous is not None:
        aliases = {len(operands) + k: k for k in range(parts)}
        operands += previous
    return pl.pallas_call(
        functools.partial(near_kernel, parts),
        grid=(count,),
        in_specs=[scalars]
        + [resident(operand.shape) for operand in operands[1:4]]
        + [row_of] * 3
        + [pl.BlockSpec((3, 1, planes, cells), lambda i: (0, i, 0, 0))] * (parts - 1)
        + [unread()] * len(aliases),
        out_specs=[row_of] + [row_one] * (parts - 1),
        out_shape=[jax.ShapeDtypeStruct(base.shape, BF16)]
        + [jax.ShapeDtypeStruct((rows, planes, cells), BF16)] * (parts - 1),
        input_output_aliases=aliases,
        compiler_params=params(),
        cost_estimate=cost(
            18 * count * planes * cells * (cells + parts * planes), 6 * count * planes * cells * (4 + parts)
        ),
        name="near",
    )(*operands)


def finish_kernel(partials, planes, profile_ref, stream_ref, home_ref, near_ref, *refs):
    partial_refs = refs[:partials]
    out_ref, turned, strips, slopes = refs[-4:]
    owners, length, cells = home_ref.shape
    rows = out_ref.shape[1]
    width = owners * planes
    held = length - 3 * planes * rows
    pitch = held // planes
    for owner in range(owners):
        strips[owner * held : (owner + 1) * held, :] = home_ref[owner, 3 * planes * rows :, :].astype(F32)
    slope = jnp.dot(strips[...].astype(BF16), stream_ref[...], preferred_element_type=F32)
    for part in range(cells // LANES):
        lanes = pl.ds(part * LANES, LANES)
        slopes[...] = slope[:, part * LANES : (part + 1) * LANES]
        lower = slopes[pl.ds(0, width, stride=pitch), :]
        upper = slopes[pl.ds(1, width, stride=pitch), :]
        for component in range(3):
            slot = component % 2
            for plane in range(width):
                place = (3 * (plane % planes) + component) * rows
                turned[slot, plane * rows : (plane + 1) * rows, :] = home_ref[
                    plane // planes, place : place + rows, lanes
                ].astype(F32)
            for row in range(rows):
                total = turned[slot, pl.ds(row, width, stride=rows), :]
                total += near_ref[component, row, :, lanes].astype(F32)
                if component == 0:
                    total += profile_ref[0, row] * lower + profile_ref[1, row] * upper
                if component == 2:
                    for ref in partial_refs:
                        total += ref[row, :, lanes].astype(F32)
                out_ref[component, row, :, lanes] = total.astype(BF16)


def finish(profile, stream, home, near_term, partials, previous, first, planes, width):
    owners, length, cells = home.shape
    rows = near_term.shape[1]
    start = first // width
    held = width // planes
    field = pl.BlockSpec((3, rows, width, cells), lambda i: (0, 0, start + i, 0))
    single = pl.BlockSpec((rows, width, cells), lambda i: (0, start + i, 0))
    operands = [profile, stream, home, near_term, *partials]
    specs = [
        pl.BlockSpec(memory_space=pltpu.SMEM),
        resident(stream.shape),
        pl.BlockSpec((held, length, cells), lambda i: (i, 0, 0)),
        field,
    ] + [single] * len(partials)
    aliases = {}
    if previous is not None:
        aliases = {len(operands): 0}
        operands.append(previous)
        specs.append(unread())
    return pl.pallas_call(
        functools.partial(finish_kernel, len(partials), planes),
        grid=(owners * planes // width,),
        in_specs=specs,
        out_specs=field,
        out_shape=jax.ShapeDtypeStruct(near_term.shape, BF16),
        scratch_shapes=[
            pltpu.VMEM((2, rows * width, LANES), F32),
            pltpu.VMEM((held * strip_rows(planes), cells), F32),
            pltpu.VMEM((held * strip_rows(planes), LANES), F32),
        ],
        input_output_aliases=aliases,
        compiler_params=params(),
        cost_estimate=cost(0, 22 * owners * planes * rows * cells),
        name="finish",
    )(*operands)


def joined_blocks(blocks, cells):
    count = cells // blocks.shape[1]
    columns = []
    for column in range(count):
        rows = [jnp.zeros(blocks.shape[1:], blocks.dtype)] * count
        for k in range(3):
            rows[(column + k - 1) % count] = rows[(column + k - 1) % count] + blocks[k]
        columns.append(jnp.concatenate(rows, axis=0))
    return jnp.concatenate(columns, axis=1)


def divide(planes):
    if planes < 2:
        return [planes]
    return [planes - planes // 2, planes // 2]


def per_device(
    base_velocity,
    velocity_step,
    adjoint_velocity,
    increment_weight,
    streamwise_first,
    streamwise_second,
    normal_first,
    normal_second,
    spanwise_first,
    spanwise_second,
    wall_profile,
):
    _, rows, planes, cells = base_velocity.shape
    owners = normal_first.shape[0] // rows
    parts = spanwise_first.shape[0] // planes
    width = 16
    slab = lax.axis_index("col")

    def from_others(start, count):
        piece = lax.slice_in_dim(adjoint_velocity, start, start + count, axis=1)
        return [
            lax.ppermute(piece, "col", [((i + shift) % parts, i) for i in range(parts)])
            for shift in range(1, parts)
        ]

    half = rows // 2
    others = [from_others(0, half), from_others(half, half)]

    chunks = divide(planes // owners)
    starts = [owners * sum(chunks[:k]) for k in range(len(chunks))]
    sent = []
    for chunk, start in zip(chunks, starts):
        block = prepare(
            increment_weight,
            base_velocity,
            velocity_step,
            adjoint_velocity,
            others[0] if sent else [],
            start,
            owners * chunk,
            width,
        )
        sent.append(block.reshape(owners, chunk, 6, rows, cells))

    received = [lax.all_to_all(block, "row", 0, 0, tiled=True) for block in sent]

    stream_first = joined_blocks(streamwise_first, cells)
    stream_second = joined_blocks(streamwise_second, cells)
    stream = jnp.concatenate([stream_first, stream_second], axis=1)

    def own_first(operator):
        return lax.dynamic_slice_in_dim(operator, slab * planes, planes, 0)

    def turned(operator, axis):
        return jnp.roll(operator, -slab * planes, axis=axis)

    curve = turned(jnp.concatenate([own_first(spanwise_first), own_first(spanwise_second)], axis=0), 1)
    cross = turned(lax.dynamic_slice_in_dim(spanwise_first, slab * planes, planes, 1), 0)
    local = None
    for number, pieces in enumerate(others):
        local = near(
            increment_weight,
            stream,
            curve,
            cross,
            base_velocity,
            velocity_step,
            adjoint_velocity,
            pieces,
            local,
            number * half,
        )
    near_term, *partials = local
    partials = [
        lax.ppermute(partial, "col", [(i, (i + shift) % parts) for i in range(parts)])
        for shift, partial in enumerate(partials, 1)
    ]

    returned = []
    for number, block in enumerate(received):
        earlier = others[1] if number == 0 else [near_term]
        term = normal(normal_first, normal_second, block, earlier)
        returned.append(lax.all_to_all(term, "row", 0, 0, tiled=True))
    result = None
    for block, start, chunk in zip(returned, starts, chunks):
        result = finish(
            wall_profile, stream_first, block, near_term, partials, result, start, chunk, width
        )
    return result


def solution(mesh):
    placed = (
        P(None, "row", "col", None),
        P(None, "row", "col", None),
        P(None, "row", "col", None),
        P(),
        P(),
        P(),
        P(),
        P(),
        P(),
        P(),
        P(None, "row"),
    )
    return jax.shard_map(
        per_device,
        mesh=mesh,
        in_specs=placed,
        out_specs=P(None, "row", "col", None),
        check_vma=False,
    )
```

```python
import functools

import jax
import jax.numpy as jnp
from jax import lax
from jax.experimental import pallas as pl
from jax.experimental.pallas import tpu as pltpu
from jax.sharding import PartitionSpec as P

F32 = jnp.float32
BF16 = jnp.bfloat16
LANES = 128
VMEM_LIMIT = 56 * 1024 * 1024


def params():
    return pltpu.CompilerParams(vmem_limit_bytes=VMEM_LIMIT)


def cost(flops, bytes_accessed):
    return pl.CostEstimate(flops=flops, bytes_accessed=bytes_accessed, transcendentals=0)


def resident(shape):
    return pl.BlockSpec(shape, lambda *_: (0,) * len(shape))


def unread():
    return pl.BlockSpec(memory_space=pl.ANY)


def mixed(weight, base, step):
    return (base.astype(F32) + weight * step.astype(F32)).astype(BF16)


def prepare_kernel(weight_ref, base_ref, step_ref, adjoint_ref, *refs):
    sent_ref = refs[-1]
    cells = base_ref.shape[3]
    weight = weight_ref[0]
    for part in range(cells // LANES):
        lanes = pl.ds(part * LANES, LANES)
        for field in range(6):
            component = field % 3
            if field < 3:
                value = mixed(weight, base_ref[component, :, :, lanes], step_ref[component, :, :, lanes])
            else:
                value = adjoint_ref[component, :, :, lanes]
            sent_ref[:, field, :, lanes] = jnp.swapaxes(value, 0, 1)


def prepare(weight, base, step, adjoint, earlier, first, count, width):
    _, rows, _, cells = base.shape
    start = first // width
    source = pl.BlockSpec((3, rows, width, cells), lambda i: (0, 0, start + i, 0))
    scalars = pl.BlockSpec(memory_space=pltpu.SMEM)
    return pl.pallas_call(
        prepare_kernel,
        grid=(count // width,),
        in_specs=[scalars, source, source, source] + [unread()] * len(earlier),
        out_specs=pl.BlockSpec((width, 6, rows, cells), lambda i: (i, 0, 0, 0)),
        out_shape=jax.ShapeDtypeStruct((count, 6, rows, cells), BF16),
        compiler_params=params(),
        cost_estimate=cost(0, 30 * count * rows * cells),
        name="prepare",
    )(weight, base, step, adjoint, *earlier)


def strip_rows(planes):
    return next(total for total in range(8, 16 * planes + 8, 8) if total % planes == 0 and total >= 2 * planes)


def normal_kernel(planes, first_ref, second_ref, lines_ref, *refs):
    out_ref, strips = refs[-2:]
    owners, _, _, rows, cells = lines_ref.shape
    lines = owners * rows
    plane = pl.program_id(0)

    def whole(field):
        return lines_ref[:, 0, field].reshape(lines, cells)

    @pl.when(plane == 0)
    def _():
        strips[...] = jnp.zeros_like(strips)

    first = first_ref[...]
    second = second_ref[...]
    cross = None
    for component in range(3):
        slope = jnp.dot(first, whole(component), preferred_element_type=F32)
        if component == 0:
            place = plane * (strips.shape[0] // planes)
            strips[pl.ds(place, 1), :] = slope[:1]
            strips[pl.ds(place + 1, 1), :] = slope[lines - 1 :]
        term = whole(3 + component).astype(F32) * slope
        cross = term if cross is None else cross + term
    speed = whole(1).astype(F32)
    for component in range(3):
        field = whole(3 + component)
        slope = jnp.dot(first, field, preferred_element_type=F32)
        term = jnp.dot(second, field, preferred_element_type=F32) - speed * slope
        if component == 1:
            term = term + cross
        place = pl.multiple_of((3 * plane + component) * rows, rows)
        out_ref[:, pl.ds(place, rows), :] = term.astype(BF16).reshape(owners, rows, cells)

    @pl.when(plane == planes - 1)
    def _():
        last = strips[...].astype(BF16)
        for owner in range(owners):
            out_ref[owner, 3 * planes * rows :, :] = last


def normal(first_op, second_op, received, earlier):
    owners, planes, _, rows, cells = received.shape
    lines = owners * rows
    length = 3 * planes * rows + strip_rows(planes)
    return pl.pallas_call(
        functools.partial(normal_kernel, planes),
        grid=(planes,),
        in_specs=[
            resident((lines, lines)),
            resident((lines, lines)),
            pl.BlockSpec((owners, 1, 6, rows, cells), lambda p: (0, p, 0, 0, 0)),
        ]
        + [unread()] * len(earlier),
        out_specs=resident((owners, length, cells)),
        out_shape=jax.ShapeDtypeStruct((owners, length, cells), BF16),
        scratch_shapes=[pltpu.VMEM((strip_rows(planes), cells), F32)],
        compiler_params=params(),
        cost_estimate=cost(18 * planes * lines * lines * cells, 18 * planes * lines * cells),
        name="normal",
    )(first_op, second_op, received, *earlier)


def near_kernel(parts, weight_ref, stream_ref, curve_ref, cross_ref, base_ref, step_ref, *refs):
    adjoint_refs = refs[:parts]
    near_ref = refs[-parts]
    partial_refs = refs[len(refs) - parts + 1 :]
    _, _, planes, cells = base_ref.shape
    weight = weight_ref[0]
    stream = stream_ref[...]
    curve = curve_ref[...]
    speeds = [mixed(weight, base_ref[c, 0], step_ref[c, 0]) for c in range(3)]
    adjoints = [[ref[c, 0] for ref in adjoint_refs] for c in range(3)]
    stream_cross = None
    span_cross = [None] * parts
    for c in range(3):
        slope = jnp.dot(speeds[c], stream[:, :cells], preferred_element_type=F32)
        term = adjoints[c][0].astype(F32) * slope
        stream_cross = term if stream_cross is None else stream_cross + term
        slopes = jnp.dot(cross_ref[...], speeds[c], preferred_element_type=F32)
        for part in range(parts):
            term = adjoints[c][part].astype(F32) * slopes[part * planes : (part + 1) * planes]
            span_cross[part] = term if span_cross[part] is None else span_cross[part] + term
    for part in range(1, parts):
        partial_refs[part - 1][0] = span_cross[part].astype(BF16)
    for c in range(3):
        along = jnp.dot(adjoints[c][0], stream, preferred_element_type=F32)
        total = along[:, cells:] - speeds[0].astype(F32) * along[:, :cells]
        across = jnp.dot(curve, jnp.concatenate(adjoints[c], axis=0), preferred_element_type=F32)
        total += across[planes:] - speeds[2].astype(F32) * across[:planes]
        if c == 0:
            total += stream_cross
        if c == 2:
            total += span_cross[0]
        near_ref[c, 0] = total.astype(BF16)


def near(weight, stream, curve, cross, base, step, own, others, previous, first):
    _, rows, planes, cells = base.shape
    parts = 1 + len(others)
    count = rows if not others else others[0].shape[1]
    row_of = pl.BlockSpec((3, 1, planes, cells), lambda i: (0, first + i, 0, 0))
    row_one = pl.BlockSpec((1, planes, cells), lambda i: (first + i, 0, 0))
    scalars = pl.BlockSpec(memory_space=pltpu.SMEM)
    operands = [weight, stream, curve, cross, base, step, own, *others]
    aliases = {}
    if previous is not None:
        aliases = {len(operands) + k: k for k in range(parts)}
        operands += previous
    return pl.pallas_call(
        functools.partial(near_kernel, parts),
        grid=(count,),
        in_specs=[scalars]
        + [resident(operand.shape) for operand in operands[1:4]]
        + [row_of] * 3
        + [pl.BlockSpec((3, 1, planes, cells), lambda i: (0, i, 0, 0))] * (parts - 1)
        + [unread()] * len(aliases),
        out_specs=[row_of] + [row_one] * (parts - 1),
        out_shape=[jax.ShapeDtypeStruct(base.shape, BF16)]
        + [jax.ShapeDtypeStruct((rows, planes, cells), BF16)] * (parts - 1),
        input_output_aliases=aliases,
        compiler_params=params(),
        cost_estimate=cost(
            18 * count * planes * cells * (cells + parts * planes), 6 * count * planes * cells * (4 + parts)
        ),
        name="near",
    )(*operands)


def pitched(size):
    return size + 8 * (1 - size // 8 % 2)


def finish_kernel(partials, planes, profile_ref, stream_ref, home_ref, near_ref, *refs):
    partial_refs = refs[:partials]
    out_ref, turned, strips, slopes = refs[-4:]
    owners, length, cells = home_ref.shape
    rows = out_ref.shape[1]
    width = owners * planes
    held = length - 3 * planes * rows
    pitch = held // planes
    for owner in range(owners):
        strips[owner * held : (owner + 1) * held, :] = home_ref[owner, 3 * planes * rows :, :].astype(F32)
    slope = jnp.dot(strips[...].astype(BF16), stream_ref[...], preferred_element_type=F32)
    for part in range(cells // LANES):
        lanes = pl.ds(part * LANES, LANES)
        slopes[...] = slope[:, part * LANES : (part + 1) * LANES]
        lower = slopes[pl.ds(0, width, stride=pitch), :]
        upper = slopes[pl.ds(1, width, stride=pitch), :]
        for component in range(3):
            slot = component % 2
            for plane in range(width):
                place = (3 * (plane % planes) + component) * rows
                turned[slot, plane, :rows, :] = home_ref[
                    plane // planes, place : place + rows, lanes
                ].astype(F32)
            flat = turned.at[slot].reshape(width * pitched(rows), LANES)
            for row in range(rows):
                total = flat[pl.ds(row, width, stride=pitched(rows)), :]
                total += near_ref[component, row, :, lanes].astype(F32)
                if component == 0:
                    total += profile_ref[0, row] * lower + profile_ref[1, row] * upper
                if component == 2:
                    for ref in partial_refs:
                        total += ref[row, :, lanes].astype(F32)
                out_ref[component, row, :, lanes] = total.astype(BF16)


def finish(profile, stream, home, near_term, partials, previous, first, planes, width):
    owners, length, cells = home.shape
    rows = near_term.shape[1]
    start = first // width
    held = width // planes
    field = pl.BlockSpec((3, rows, width, cells), lambda i: (0, 0, start + i, 0))
    single = pl.BlockSpec((rows, width, cells), lambda i: (0, start + i, 0))
    operands = [profile, stream, home, near_term, *partials]
    specs = [
        pl.BlockSpec(memory_space=pltpu.SMEM),
        resident(stream.shape),
        pl.BlockSpec((held, length, cells), lambda i: (i, 0, 0)),
        field,
    ] + [single] * len(partials)
    aliases = {}
    if previous is not None:
        aliases = {len(operands): 0}
        operands.append(previous)
        specs.append(unread())
    return pl.pallas_call(
        functools.partial(finish_kernel, len(partials), planes),
        grid=(owners * planes // width,),
        in_specs=specs,
        out_specs=field,
        out_shape=jax.ShapeDtypeStruct(near_term.shape, BF16),
        scratch_shapes=[
            pltpu.VMEM((2, width, pitched(rows), LANES), F32),
            pltpu.VMEM((held * strip_rows(planes), cells), F32),
            pltpu.VMEM((held * strip_rows(planes), LANES), F32),
        ],
        input_output_aliases=aliases,
        compiler_params=params(),
        cost_estimate=cost(0, 22 * owners * planes * rows * cells),
        name="finish",
    )(*operands)


def joined_blocks(blocks, cells):
    count = cells // blocks.shape[1]
    columns = []
    for column in range(count):
        rows = [jnp.zeros(blocks.shape[1:], blocks.dtype)] * count
        for k in range(3):
            rows[(column + k - 1) % count] = rows[(column + k - 1) % count] + blocks[k]
        columns.append(jnp.concatenate(rows, axis=0))
    return jnp.concatenate(columns, axis=1)


def divide(planes):
    if planes < 2:
        return [planes]
    return [planes - planes // 2, planes // 2]


def step_width(start, count):
    return next(width for width in (32, 16, 8) if start % width == 0 and count % width == 0)


def per_device(
    base_velocity,
    velocity_step,
    adjoint_velocity,
    increment_weight,
    streamwise_first,
    streamwise_second,
    normal_first,
    normal_second,
    spanwise_first,
    spanwise_second,
    wall_profile,
):
    _, rows, planes, cells = base_velocity.shape
    owners = normal_first.shape[0] // rows
    parts = spanwise_first.shape[0] // planes
    slab = lax.axis_index("col")

    def from_others(start, count):
        piece = lax.slice_in_dim(adjoint_velocity, start, start + count, axis=1)
        return [
            lax.ppermute(piece, "col", [((i + shift) % parts, i) for i in range(parts)])
            for shift in range(1, parts)
        ]

    half = rows // 2
    others = [from_others(0, half), from_others(half, half)]

    chunks = divide(planes // owners)
    starts = [owners * sum(chunks[:k]) for k in range(len(chunks))]
    sent = []
    for chunk, start in zip(chunks, starts):
        block = prepare(
            increment_weight,
            base_velocity,
            velocity_step,
            adjoint_velocity,
            others[0] if sent else [],
            start,
            owners * chunk,
            16,
        )
        sent.append(block.reshape(owners, chunk, 6, rows, cells))

    received = [lax.all_to_all(block, "row", 0, 0, tiled=True) for block in sent]

    stream_first = joined_blocks(streamwise_first, cells)
    stream_second = joined_blocks(streamwise_second, cells)
    stream = jnp.concatenate([stream_first, stream_second], axis=1)

    def own_first(operator):
        return lax.dynamic_slice_in_dim(operator, slab * planes, planes, 0)

    def turned(operator, axis):
        return jnp.roll(operator, -slab * planes, axis=axis)

    curve = turned(jnp.concatenate([own_first(spanwise_first), own_first(spanwise_second)], axis=0), 1)
    cross = turned(lax.dynamic_slice_in_dim(spanwise_first, slab * planes, planes, 1), 0)
    local = None
    for number, pieces in enumerate(others):
        local = near(
            increment_weight,
            stream,
            curve,
            cross,
            base_velocity,
            velocity_step,
            adjoint_velocity,
            pieces,
            local,
            number * half,
        )
    near_term, *partials = local
    partials = [
        lax.ppermute(partial, "col", [(i, (i + shift) % parts) for i in range(parts)])
        for shift, partial in enumerate(partials, 1)
    ]

    returned = []
    for number, block in enumerate(received):
        earlier = others[1] if number == 0 else [near_term]
        term = normal(normal_first, normal_second, block, earlier)
        returned.append(lax.all_to_all(term, "row", 0, 0, tiled=True))
    result = None
    for block, start, chunk in zip(returned, starts, chunks):
        result = finish(
            wall_profile, stream_first, block, near_term, partials, result, start, chunk, step_width(start, owners * chunk)
        )
    return result


def solution(mesh):
    placed = (
        P(None, "row", "col", None),
        P(None, "row", "col", None),
        P(None, "row", "col", None),
        P(),
        P(),
        P(),
        P(),
        P(),
        P(),
        P(),
        P(None, "row"),
    )
    return jax.shard_map(
        per_device,
        mesh=mesh,
        in_specs=placed,
        out_specs=P(None, "row", "col", None),
        check_vma=False,
    )
```

```python
import functools

import jax
import jax.numpy as jnp
from jax import lax
from jax.experimental import pallas as pl
from jax.experimental.pallas import tpu as pltpu
from jax.sharding import PartitionSpec as P

F32 = jnp.float32
BF16 = jnp.bfloat16
LANES = 128
VMEM_LIMIT = 56 * 1024 * 1024


def params():
    return pltpu.CompilerParams(vmem_limit_bytes=VMEM_LIMIT)


def cost(flops, bytes_accessed):
    return pl.CostEstimate(flops=flops, bytes_accessed=bytes_accessed, transcendentals=0)


def resident(shape):
    return pl.BlockSpec(shape, lambda *_: (0,) * len(shape))


def unread():
    return pl.BlockSpec(memory_space=pl.ANY)


def mixed(weight, base, step):
    return (base.astype(F32) + weight * step.astype(F32)).astype(BF16)


def prepare_kernel(planes, profiles, weight_ref, base_ref, step_ref, adjoint_ref, *refs):
    sent_ref = refs[-1]
    rows, width, cells = base_ref.shape[1:]
    weight = weight_ref[0]
    for part in range(cells // LANES):
        lanes = pl.ds(part * LANES, LANES)
        for field in range(6):
            component = field % 3
            if field < 3:
                value = mixed(weight, base_ref[component, :, :, lanes], step_ref[component, :, :, lanes])
            else:
                value = adjoint_ref[component, :, :, lanes]
            value = jnp.swapaxes(value, 0, 1)
            for plane in range(width):
                place = (6 * (plane % planes) + field) * rows
                sent_ref[plane // planes, place : place + rows, lanes] = value[plane]
    if profiles:
        rest = refs[0][...]
        pieces = []
        for _ in range(3):
            pieces.append(rest.astype(BF16).astype(F32))
            rest = rest - pieces[-1]
        pieces.append(jnp.zeros_like(rest))
        joined = jnp.concatenate(pieces, axis=0).astype(BF16)
        for owner in range(width // planes):
            sent_ref[owner, 6 * planes * rows :, :rows] = joined


def prepare(weight, base, step, adjoint, profiles, earlier, first, owners, planes, width):
    _, rows, _, cells = base.shape
    start = first // width
    source = pl.BlockSpec((3, rows, width, cells), lambda i: (0, 0, start + i, 0))
    length = 6 * planes * rows + 8 * len(profiles)
    return pl.pallas_call(
        functools.partial(prepare_kernel, planes, len(profiles)),
        grid=(owners * planes // width,),
        in_specs=[pl.BlockSpec(memory_space=pltpu.SMEM), source, source, source]
        + [resident(profile.shape) for profile in profiles]
        + [unread()] * len(earlier),
        out_specs=pl.BlockSpec((width // planes, length, cells), lambda i: (i, 0, 0)),
        out_shape=jax.ShapeDtypeStruct((owners, length, cells), BF16),
        compiler_params=params(),
        cost_estimate=cost(0, 30 * owners * planes * rows * cells),
        name="prepare",
    )(weight, base, step, adjoint, *profiles, *earlier)


def normal_kernel(first_ref, second_ref, stream_ref, profile_ref, lines_ref, *refs):
    out_ref, strips = refs[-2:]
    owners, length, cells = lines_ref.shape
    rows = length // 6
    lines = owners * rows

    def whole(field):
        return lines_ref[:, field * rows : (field + 1) * rows, :].reshape(lines, cells)

    first = first_ref[...]
    second = second_ref[...]
    cross = None
    for component in range(3):
        slope = jnp.dot(first, whole(component), preferred_element_type=F32)
        if component == 0:
            strips[...] = jnp.zeros_like(strips)
            strips[:1, :] = slope[:1]
            strips[1:2, :] = slope[lines - 1 :]
        term = whole(3 + component).astype(F32) * slope
        cross = term if cross is None else cross + term
    wall_shear = strips[...].astype(BF16)
    shear_slope = jnp.dot(wall_shear, stream_ref[...], preferred_element_type=F32)
    speed = whole(1).astype(F32)
    for component in range(3):
        field = whole(3 + component)
        slope = jnp.dot(first, field, preferred_element_type=F32)
        term = jnp.dot(second, field, preferred_element_type=F32) - speed * slope
        if component == 0:
            term += profile_ref[:, :1] * shear_slope[:1] + profile_ref[:, 1:] * shear_slope[1:2]
        if component == 1:
            term += cross
        out_ref[:, 0, component] = term.astype(BF16).reshape(owners, rows, cells)


def normal(first_op, second_op, stream, profile, received, planes, earlier):
    owners, _, cells = received.shape
    lines = first_op.shape[0]
    rows = lines // owners
    return pl.pallas_call(
        normal_kernel,
        grid=(planes,),
        in_specs=[resident(operand.shape) for operand in (first_op, second_op, stream, profile)]
        + [pl.BlockSpec((owners, 6 * rows, cells), lambda p: (0, p, 0))]
        + [unread()] * len(earlier),
        out_specs=pl.BlockSpec((owners, 1, 3, rows, cells), lambda p: (0, p, 0, 0, 0)),
        out_shape=jax.ShapeDtypeStruct((owners, planes, 3, rows, cells), BF16),
        scratch_shapes=[pltpu.VMEM((16, cells), F32)],
        compiler_params=params(),
        cost_estimate=cost(18 * planes * lines * lines * cells, 18 * planes * lines * cells),
        name="normal",
    )(first_op, second_op, stream, profile, received, *earlier)


def near_kernel(parts, weight_ref, stream_ref, curve_ref, cross_ref, base_ref, step_ref, *refs):
    adjoint_refs = refs[:parts]
    near_ref = refs[-parts]
    partial_refs = refs[len(refs) - parts + 1 :]
    _, _, planes, cells = base_ref.shape
    weight = weight_ref[0]
    stream = stream_ref[...]
    curve = curve_ref[...]
    speeds = [mixed(weight, base_ref[c, 0], step_ref[c, 0]) for c in range(3)]
    adjoints = [[ref[c, 0] for ref in adjoint_refs] for c in range(3)]
    stream_cross = None
    span_cross = [None] * parts
    for c in range(3):
        slope = jnp.dot(speeds[c], stream[:, :cells], preferred_element_type=F32)
        term = adjoints[c][0].astype(F32) * slope
        stream_cross = term if stream_cross is None else stream_cross + term
        slopes = jnp.dot(cross_ref[...], speeds[c], preferred_element_type=F32)
        for part in range(parts):
            term = adjoints[c][part].astype(F32) * slopes[part * planes : (part + 1) * planes]
            span_cross[part] = term if span_cross[part] is None else span_cross[part] + term
    for part in range(1, parts):
        partial_refs[part - 1][0] = span_cross[part].astype(BF16)
    for c in range(3):
        along = jnp.dot(adjoints[c][0], stream, preferred_element_type=F32)
        total = along[:, cells:] - speeds[0].astype(F32) * along[:, :cells]
        across = jnp.dot(curve, jnp.concatenate(adjoints[c], axis=0), preferred_element_type=F32)
        total += across[planes:] - speeds[2].astype(F32) * across[:planes]
        if c == 0:
            total += stream_cross
        if c == 2:
            total += span_cross[0]
        near_ref[c, 0] = total.astype(BF16)


def near(weight, stream, curve, cross, base, step, own, others, previous, first, count):
    _, rows, planes, cells = base.shape
    parts = 1 + len(others)
    row_of = pl.BlockSpec((3, 1, planes, cells), lambda i: (0, first + i, 0, 0))
    row_one = pl.BlockSpec((1, planes, cells), lambda i: (first + i, 0, 0))
    scalars = pl.BlockSpec(memory_space=pltpu.SMEM)
    operands = [weight, stream, curve, cross, base, step, own, *others]
    aliases = {}
    if previous is not None:
        aliases = {len(operands) + k: k for k in range(parts)}
        operands += previous
    return pl.pallas_call(
        functools.partial(near_kernel, parts),
        grid=(count,),
        in_specs=[scalars]
        + [resident(operand.shape) for operand in operands[1:4]]
        + [row_of] * 3
        + [pl.BlockSpec((3, 1, planes, cells), lambda i: (0, i, 0, 0))] * (parts - 1)
        + [unread()] * len(aliases),
        out_specs=[row_of] + [row_one] * (parts - 1),
        out_shape=[jax.ShapeDtypeStruct(base.shape, BF16)]
        + [jax.ShapeDtypeStruct((rows, planes, cells), BF16)] * (parts - 1),
        input_output_aliases=aliases,
        compiler_params=params(),
        cost_estimate=cost(
            18 * count * planes * cells * (cells + parts * planes), 6 * count * planes * cells * (4 + parts)
        ),
        name="near",
    )(*operands)


def pitched(size):
    return size + 8 * (1 - size // 8 % 2)


def finish_kernel(partials, home_ref, near_ref, *refs):
    partial_refs = refs[:partials]
    out_ref, turned = refs[-2:]
    width, _, rows, cells = home_ref.shape
    pitch = pitched(rows)
    for part in range(cells // LANES):
        lanes = pl.ds(part * LANES, LANES)
        for component in range(3):
            slot = component % 2
            for plane in range(width):
                turned[slot, plane * pitch : plane * pitch + rows, :] = home_ref[plane, component, :, lanes].astype(
                    F32
                )
            for row in range(rows):
                total = turned[slot, pl.ds(row, width, stride=pitch), :]
                total += near_ref[component, row, :, lanes].astype(F32)
                if component == 2:
                    for ref in partial_refs:
                        total += ref[row, :, lanes].astype(F32)
                out_ref[component, row, :, lanes] = total.astype(BF16)


def finish(home, near_term, partials, previous, first, width):
    count, _, rows, cells = home.shape
    start = first // width
    field = pl.BlockSpec((3, rows, width, cells), lambda i: (0, 0, start + i, 0))
    single = pl.BlockSpec((rows, width, cells), lambda i: (0, start + i, 0))
    operands = [home, near_term, *partials]
    specs = [pl.BlockSpec((width, 3, rows, cells), lambda i: (i, 0, 0, 0)), field] + [single] * len(partials)
    aliases = {}
    if previous is not None:
        aliases = {len(operands): 0}
        operands.append(previous)
        specs.append(unread())
    return pl.pallas_call(
        functools.partial(finish_kernel, len(partials)),
        grid=(count // width,),
        in_specs=specs,
        out_specs=field,
        out_shape=jax.ShapeDtypeStruct(near_term.shape, BF16),
        scratch_shapes=[pltpu.VMEM((2, width * pitched(rows), LANES), F32)],
        input_output_aliases=aliases,
        compiler_params=params(),
        cost_estimate=cost(0, 22 * count * rows * cells),
        name="finish",
    )(*operands)


def joined_blocks(blocks, cells):
    count = cells // blocks.shape[1]
    columns = []
    for column in range(count):
        rows = [jnp.zeros(blocks.shape[1:], blocks.dtype)] * count
        for k in range(3):
            rows[(column + k - 1) % count] = rows[(column + k - 1) % count] + blocks[k]
        columns.append(jnp.concatenate(rows, axis=0))
    return jnp.concatenate(columns, axis=1)


def divide(planes):
    if planes < 2:
        return [planes]
    return [planes - planes // 2, planes // 2]


def step_width(start, count):
    return next(width for width in (32, 16, 8) if start % width == 0 and count % width == 0)


def per_device(
    base_velocity,
    velocity_step,
    adjoint_velocity,
    increment_weight,
    streamwise_first,
    streamwise_second,
    normal_first,
    normal_second,
    spanwise_first,
    spanwise_second,
    wall_profile,
):
    _, rows, planes, cells = base_velocity.shape
    owners = normal_first.shape[0] // rows
    parts = spanwise_first.shape[0] // planes
    slab = lax.axis_index("col")

    def from_others(start, count):
        piece = lax.slice_in_dim(adjoint_velocity, start, start + count, axis=1)
        return [
            lax.ppermute(piece, "col", [((i + shift) % parts, i) for i in range(parts)])
            for shift in range(1, parts)
        ]

    half = rows // 2
    others = [from_others(0, half), from_others(half, half)]

    chunks = divide(planes // owners)
    starts = [owners * sum(chunks[:k]) for k in range(len(chunks))]
    sent = []
    for number, (chunk, start) in enumerate(zip(chunks, starts)):
        sent.append(
            prepare(
                increment_weight,
                base_velocity,
                velocity_step,
                adjoint_velocity,
                [wall_profile] if number == 0 else [],
                others[0] if number == 1 else [],
                start,
                owners,
                chunk,
                16,
            )
        )

    received = [lax.all_to_all(block, "row", 0, 0, tiled=True) for block in sent]

    pieces = received[0][:, 6 * chunks[0] * rows :, :rows].astype(F32)
    profile = (pieces[:, 0:2] + pieces[:, 2:4] + pieces[:, 4:6]).transpose(0, 2, 1).reshape(owners * rows, 2)
    stream_first = joined_blocks(streamwise_first, cells)
    stream_second = joined_blocks(streamwise_second, cells)
    stream = jnp.concatenate([stream_first, stream_second], axis=1)

    def own_first(operator):
        return lax.dynamic_slice_in_dim(operator, slab * planes, planes, 0)

    def turned(operator, axis):
        return jnp.roll(operator, -slab * planes, axis=axis)

    curve = turned(jnp.concatenate([own_first(spanwise_first), own_first(spanwise_second)], axis=0), 1)
    cross = turned(lax.dynamic_slice_in_dim(spanwise_first, slab * planes, planes, 1), 0)
    local = None
    for number, pieces in enumerate(others):
        local = near(
            increment_weight,
            stream,
            curve,
            cross,
            base_velocity,
            velocity_step,
            adjoint_velocity,
            pieces,
            local,
            number * half,
            half,
        )
    near_term, *partials = local
    partials = [
        lax.ppermute(partial, "col", [(i, (i + shift) % parts) for i in range(parts)])
        for shift, partial in enumerate(partials, 1)
    ]

    returned = []
    for number, (block, chunk) in enumerate(zip(received, chunks)):
        earlier = others[1] if number == 0 else [near_term]
        term = normal(normal_first, normal_second, stream_first, profile, block, chunk, earlier)
        returned.append(lax.all_to_all(term, "row", 0, 0, tiled=True))
    result = None
    for block, start, chunk in zip(returned, starts, chunks):
        home = block.reshape(owners * chunk, 3, rows, cells)
        width = step_width(start, owners * chunk)
        result = finish(home, near_term, partials, result, start, width)
    return result


def solution(mesh):
    placed = (
        P(None, "row", "col", None),
        P(None, "row", "col", None),
        P(None, "row", "col", None),
        P(),
        P(),
        P(),
        P(),
        P(),
        P(),
        P(),
        P(None, "row"),
    )
    return jax.shard_map(
        per_device,
        mesh=mesh,
        in_specs=placed,
        out_specs=P(None, "row", "col", None),
        check_vma=False,
    )
```

```python
import functools

import jax
import jax.numpy as jnp
from jax import lax
from jax.experimental import pallas as pl
from jax.experimental.pallas import tpu as pltpu
from jax.sharding import PartitionSpec as P

F32 = jnp.float32
BF16 = jnp.bfloat16
LANES = 128
VMEM_LIMIT = 56 * 1024 * 1024


def params():
    return pltpu.CompilerParams(vmem_limit_bytes=VMEM_LIMIT)


def cost(flops, bytes_accessed):
    return pl.CostEstimate(flops=flops, bytes_accessed=bytes_accessed, transcendentals=0)


def resident(shape):
    return pl.BlockSpec(shape, lambda *_: (0,) * len(shape))


def unread():
    return pl.BlockSpec(memory_space=pl.ANY)


def mixed(weight, base, step):
    return (base.astype(F32) + weight * step.astype(F32)).astype(BF16)


def prepare_kernel(planes, profiles, weight_ref, base_ref, step_ref, adjoint_ref, *refs):
    sent_ref = refs[-1]
    rows, width, cells = base_ref.shape[1:]
    weight = weight_ref[0]
    for part in range(cells // LANES):
        lanes = pl.ds(part * LANES, LANES)
        for field in range(6):
            component = field % 3
            if field < 3:
                value = mixed(weight, base_ref[component, :, :, lanes], step_ref[component, :, :, lanes])
            else:
                value = adjoint_ref[component, :, :, lanes]
            value = jnp.swapaxes(value, 0, 1)
            for plane in range(width):
                place = (6 * (plane % planes) + field) * rows
                sent_ref[plane // planes, place : place + rows, lanes] = value[plane]
    if profiles:
        rest = refs[0][...]
        pieces = []
        for _ in range(3):
            pieces.append(rest.astype(BF16).astype(F32))
            rest = rest - pieces[-1]
        pieces.append(jnp.zeros_like(rest))
        joined = jnp.concatenate(pieces, axis=0).astype(BF16)
        for owner in range(width // planes):
            sent_ref[owner, 6 * planes * rows :, :rows] = joined


def prepare(weight, base, step, adjoint, profiles, earlier, first, owners, planes, width):
    _, rows, _, cells = base.shape
    start = first // width
    source = pl.BlockSpec((3, rows, width, cells), lambda i: (0, 0, start + i, 0))
    length = 6 * planes * rows + 8 * len(profiles)
    return pl.pallas_call(
        functools.partial(prepare_kernel, planes, len(profiles)),
        grid=(owners * planes // width,),
        in_specs=[pl.BlockSpec(memory_space=pltpu.SMEM), source, source, source]
        + [resident(profile.shape) for profile in profiles]
        + [unread()] * len(earlier),
        out_specs=pl.BlockSpec((width // planes, length, cells), lambda i: (i, 0, 0)),
        out_shape=jax.ShapeDtypeStruct((owners, length, cells), BF16),
        compiler_params=params(),
        cost_estimate=cost(0, 30 * owners * planes * rows * cells),
        name="prepare",
    )(weight, base, step, adjoint, *profiles, *earlier)


def normal_kernel(first_ref, second_ref, stream_ref, profile_ref, lines_ref, *refs):
    out_ref, strips = refs[-2:]
    owners, length, cells = lines_ref.shape
    rows = length // 6
    lines = owners * rows

    def whole(field):
        return lines_ref[:, field * rows : (field + 1) * rows, :].reshape(lines, cells)

    first = first_ref[...]
    second = second_ref[...]
    cross = None
    for component in range(3):
        slope = jnp.dot(first, whole(component), preferred_element_type=F32)
        if component == 0:
            strips[...] = jnp.zeros_like(strips)
            strips[:1, :] = slope[:1]
            strips[1:2, :] = slope[lines - 1 :]
        term = whole(3 + component).astype(F32) * slope
        cross = term if cross is None else cross + term
    wall_shear = strips[...].astype(BF16)
    shear_slope = jnp.dot(wall_shear, stream_ref[...], preferred_element_type=F32)
    speed = whole(1).astype(F32)
    for component in range(3):
        field = whole(3 + component)
        slope = jnp.dot(first, field, preferred_element_type=F32)
        term = jnp.dot(second, field, preferred_element_type=F32) - speed * slope
        if component == 0:
            term += profile_ref[:, :1] * shear_slope[:1] + profile_ref[:, 1:] * shear_slope[1:2]
        if component == 1:
            term += cross
        out_ref[:, 0, component] = term.astype(BF16).reshape(owners, rows, cells)


def normal(first_op, second_op, stream, profile, received, planes, earlier):
    owners, _, cells = received.shape
    lines = first_op.shape[0]
    rows = lines // owners
    return pl.pallas_call(
        normal_kernel,
        grid=(planes,),
        in_specs=[resident(operand.shape) for operand in (first_op, second_op, stream, profile)]
        + [pl.BlockSpec((owners, 6 * rows, cells), lambda p: (0, p, 0))]
        + [unread()] * len(earlier),
        out_specs=pl.BlockSpec((owners, 1, 3, rows, cells), lambda p: (0, p, 0, 0, 0)),
        out_shape=jax.ShapeDtypeStruct((owners, planes, 3, rows, cells), BF16),
        scratch_shapes=[pltpu.VMEM((16, cells), F32)],
        compiler_params=params(),
        cost_estimate=cost(18 * planes * lines * lines * cells, 18 * planes * lines * cells),
        name="normal",
    )(first_op, second_op, stream, profile, received, *earlier)


def near_kernel(parts, weight_ref, stream_ref, curve_ref, cross_ref, base_ref, step_ref, *refs):
    adjoint_refs = refs[:parts]
    near_ref = refs[-parts]
    partial_refs = refs[len(refs) - parts + 1 :]
    _, _, planes, cells = base_ref.shape
    weight = weight_ref[0]
    stream = stream_ref[...]
    curve = curve_ref[...]
    speeds = [mixed(weight, base_ref[c, 0], step_ref[c, 0]) for c in range(3)]
    adjoints = [[ref[c, 0] for ref in adjoint_refs] for c in range(3)]
    stream_cross = None
    span_cross = [None] * parts
    for c in range(3):
        slope = jnp.dot(speeds[c], stream[:, :cells], preferred_element_type=F32)
        term = adjoints[c][0].astype(F32) * slope
        stream_cross = term if stream_cross is None else stream_cross + term
        slopes = jnp.dot(cross_ref[...], speeds[c], preferred_element_type=F32)
        for part in range(parts):
            term = adjoints[c][part].astype(F32) * slopes[part * planes : (part + 1) * planes]
            span_cross[part] = term if span_cross[part] is None else span_cross[part] + term
    for part in range(1, parts):
        partial_refs[part - 1][0] = span_cross[part].astype(BF16)
    for c in range(3):
        along = jnp.dot(adjoints[c][0], stream, preferred_element_type=F32)
        total = along[:, cells:] - speeds[0].astype(F32) * along[:, :cells]
        across = jnp.dot(curve, jnp.concatenate(adjoints[c], axis=0), preferred_element_type=F32)
        total += across[planes:] - speeds[2].astype(F32) * across[:planes]
        if c == 0:
            total += stream_cross
        if c == 2:
            total += span_cross[0]
        near_ref[c, 0] = total.astype(BF16)


def near(weight, stream, curve, cross, base, step, own, others, previous, first, count):
    _, rows, planes, cells = base.shape
    parts = 1 + len(others)
    row_of = pl.BlockSpec((3, 1, planes, cells), lambda i: (0, first + i, 0, 0))
    row_one = pl.BlockSpec((1, planes, cells), lambda i: (first + i, 0, 0))
    scalars = pl.BlockSpec(memory_space=pltpu.SMEM)
    operands = [weight, stream, curve, cross, base, step, own, *others]
    aliases = {}
    if previous is not None:
        aliases = {len(operands) + k: k for k in range(parts)}
        operands += previous
    return pl.pallas_call(
        functools.partial(near_kernel, parts),
        grid=(count,),
        in_specs=[scalars]
        + [resident(operand.shape) for operand in operands[1:4]]
        + [row_of] * 3
        + [pl.BlockSpec((3, 1, planes, cells), lambda i: (0, i, 0, 0))] * (parts - 1)
        + [unread()] * len(aliases),
        out_specs=[row_of] + [row_one] * (parts - 1),
        out_shape=[jax.ShapeDtypeStruct(base.shape, BF16)]
        + [jax.ShapeDtypeStruct((rows, planes, cells), BF16)] * (parts - 1),
        input_output_aliases=aliases,
        compiler_params=params(),
        cost_estimate=cost(
            18 * count * planes * cells * (cells + parts * planes), 6 * count * planes * cells * (4 + parts)
        ),
        name="near",
    )(*operands)


def pitched(size):
    return size + 8 * (1 - size // 8 % 2)


def finish_kernel(partials, home_ref, near_ref, *refs):
    partial_refs = refs[:partials]
    out_ref, turned = refs[-2:]
    width, _, rows, cells = home_ref.shape
    pitch = pitched(rows)
    for part in range(cells // LANES):
        lanes = pl.ds(part * LANES, LANES)
        for component in range(3):
            slot = component % 2
            for plane in range(width):
                turned[slot, plane * pitch : plane * pitch + rows, :] = home_ref[plane, component, :, lanes].astype(
                    F32
                )
            for row in range(rows):
                total = turned[slot, pl.ds(row, width, stride=pitch), :]
                total += near_ref[component, row, :, lanes].astype(F32)
                if component == 2:
                    for ref in partial_refs:
                        total += ref[row, :, lanes].astype(F32)
                out_ref[component, row, :, lanes] = total.astype(BF16)


def finish(home, near_term, partials, previous, first, width):
    count, _, rows, cells = home.shape
    start = first // width
    field = pl.BlockSpec((3, rows, width, cells), lambda i: (0, 0, start + i, 0))
    single = pl.BlockSpec((rows, width, cells), lambda i: (0, start + i, 0))
    operands = [home, near_term, *partials]
    specs = [pl.BlockSpec((width, 3, rows, cells), lambda i: (i, 0, 0, 0)), field] + [single] * len(partials)
    aliases = {}
    if previous is not None:
        aliases = {len(operands): 0}
        operands.append(previous)
        specs.append(unread())
    return pl.pallas_call(
        functools.partial(finish_kernel, len(partials)),
        grid=(count // width,),
        in_specs=specs,
        out_specs=field,
        out_shape=jax.ShapeDtypeStruct(near_term.shape, BF16),
        scratch_shapes=[pltpu.VMEM((2, width * pitched(rows), LANES), F32)],
        input_output_aliases=aliases,
        compiler_params=params(),
        cost_estimate=cost(0, 22 * count * rows * cells),
        name="finish",
    )(*operands)


def joined_blocks(blocks, cells):
    count = cells // blocks.shape[1]
    columns = []
    for column in range(count):
        rows = [jnp.zeros(blocks.shape[1:], blocks.dtype)] * count
        for k in range(3):
            rows[(column + k - 1) % count] = rows[(column + k - 1) % count] + blocks[k]
        columns.append(jnp.concatenate(rows, axis=0))
    return jnp.concatenate(columns, axis=1)


def divide(planes):
    if planes < 2:
        return [planes]
    return [planes - planes // 2, planes // 2]


def step_width(start, count):
    return next(width for width in (32, 16, 8) if start % width == 0 and count % width == 0)


def per_device(
    base_velocity,
    velocity_step,
    adjoint_velocity,
    increment_weight,
    streamwise_first,
    streamwise_second,
    normal_first,
    normal_second,
    spanwise_first,
    spanwise_second,
    wall_profile,
):
    _, rows, planes, cells = base_velocity.shape
    owners = normal_first.shape[0] // rows
    parts = spanwise_first.shape[0] // planes
    slab = lax.axis_index("col")

    def from_others(start, count):
        piece = lax.slice_in_dim(adjoint_velocity, start, start + count, axis=1)
        return [
            lax.ppermute(piece, "col", [((i + shift) % parts, i) for i in range(parts)])
            for shift in range(1, parts)
        ]

    half = rows // 2
    others = [from_others(0, half), from_others(half, half)]

    chunks = divide(planes // owners)
    starts = [owners * sum(chunks[:k]) for k in range(len(chunks))]
    sent = []
    for number, (chunk, start) in enumerate(zip(chunks, starts)):
        sent.append(
            prepare(
                increment_weight,
                base_velocity,
                velocity_step,
                adjoint_velocity,
                [wall_profile] if number == 0 else [],
                others[0] if number == 1 else [],
                start,
                owners,
                chunk,
                step_width(start, owners * chunk),
            )
        )

    received = [lax.all_to_all(block, "row", 0, 0, tiled=True) for block in sent]

    pieces = received[0][:, 6 * chunks[0] * rows :, :rows].astype(F32)
    profile = (pieces[:, 0:2] + pieces[:, 2:4] + pieces[:, 4:6]).transpose(0, 2, 1).reshape(owners * rows, 2)
    stream_first = joined_blocks(streamwise_first, cells)
    stream_second = joined_blocks(streamwise_second, cells)
    stream = jnp.concatenate([stream_first, stream_second], axis=1)

    def own_first(operator):
        return lax.dynamic_slice_in_dim(operator, slab * planes, planes, 0)

    def turned(operator, axis):
        return jnp.roll(operator, -slab * planes, axis=axis)

    curve = turned(jnp.concatenate([own_first(spanwise_first), own_first(spanwise_second)], axis=0), 1)
    cross = turned(lax.dynamic_slice_in_dim(spanwise_first, slab * planes, planes, 1), 0)
    local = None
    for number, pieces in enumerate(others):
        local = near(
            increment_weight,
            stream,
            curve,
            cross,
            base_velocity,
            velocity_step,
            adjoint_velocity,
            pieces,
            local,
            number * half,
            half,
        )
    near_term, *partials = local
    partials = [
        lax.ppermute(partial, "col", [(i, (i + shift) % parts) for i in range(parts)])
        for shift, partial in enumerate(partials, 1)
    ]

    returned = []
    for number, (block, chunk) in enumerate(zip(received, chunks)):
        earlier = others[1] if number == 0 else [near_term]
        term = normal(normal_first, normal_second, stream_first, profile, block, chunk, earlier)
        returned.append(lax.all_to_all(term, "row", 0, 0, tiled=True))
    result = None
    for block, start, chunk in zip(returned, starts, chunks):
        home = block.reshape(owners * chunk, 3, rows, cells)
        width = step_width(start, owners * chunk)
        result = finish(home, near_term, partials, result, start, width)
    return result


def solution(mesh):
    placed = (
        P(None, "row", "col", None),
        P(None, "row", "col", None),
        P(None, "row", "col", None),
        P(),
        P(),
        P(),
        P(),
        P(),
        P(),
        P(),
        P(None, "row"),
    )
    return jax.shard_map(
        per_device,
        mesh=mesh,
        in_specs=placed,
        out_specs=P(None, "row", "col", None),
        check_vma=False,
    )
```
